32 devices in a mesh: row: 4 (over z), col: 8 (over y, x, core).
Axes of the slice: x: 2, y: 2, z: 4, core: 2. Of those that a mesh axis runs over, the one named last changes fastest.
Arguments:
- amplitudes: bfloat16 [512, 8, 4096], P('col', None, 'row'), may hold values from -6 to 6
- integrals: bfloat16 [32, 4096, 4096], P(None, 'row', 'col'), may hold values from -0.046875 to 0.046875
- blocks: int32 [32, 2], replicated, may hold values from 0 to 7, as said below
Outputs:
- ladder: bfloat16 [512, 8, 4096], P(('row', 'col'))
The draws below stay inside these ranges and needn't reach their ends.
Inputs may be any that keep to these rules, and one draw needn't show every extreme that they name: No (contracted tile, output tile) pair appears twice; each of the 8 contracted tiles and each output tile appears in exactly 4 blocks.
All inputs are finite; a program needn't handle non-finite values.
Results may differ from the reference program's by a relative error of at most 0.001.
Values may be sent and summed in bfloat16 or wider, within the bound.
A program may use at most 192 MiB of HBM per device.

```python
import jax
import jax.numpy as jnp
from jax import lax

PAIR_WIDTH = 4096
PAIR_TILES = 8
BLOCKS = 32
BLK_PER_Q = 4
PAIRS = 512


def draw_blocks(key, part):
    key_rows, key_cols, key_shuffle = jax.random.split(jax.random.fold_in(key, 17), 3)
    row_perm = jax.random.permutation(key_rows, PAIR_TILES)
    col_perm = jax.random.permutation(key_cols, PAIR_TILES)
    lanes = jnp.arange(BLOCKS) % PAIR_TILES
    turns = jnp.arange(BLOCKS) // PAIR_TILES
    table = jnp.stack([row_perm[lanes], col_perm[(lanes + turns) % PAIR_TILES]], axis=1)
    shuffle = jax.random.permutation(key_shuffle, BLOCKS)
    return table[shuffle].astype(jnp.int32)


def block_levels(stream_key, dims, cuts, least, top_value):
    def one(position, shards_of):
        draws = jax.random.uniform(jax.random.fold_in(jax.random.fold_in(stream_key, 6), position), (shards_of,), jnp.float32, least / len(cuts), top_value / len(cuts))
        return jnp.repeat(jnp.exp(draws), dims[position] // shards_of).reshape((-1,) + (1,) * (len(dims) - position - 1))

    level = one(*cuts[0])
    for cut in cuts[1:]:
        level = level * one(*cut)
    return level


def normal_values(key, extent, deviation, bound, shards=(), held_as=jnp.bfloat16):
    gain = block_levels(key, extent, shards, -0.22, 0.18) if shards else 1.0
    array = jax.random.normal(key, extent, jnp.float32) * deviation * gain
    return jnp.minimum(jnp.maximum(array, -bound), bound).astype(held_as)


def setup_inputs(seed: int = 0) -> dict:
    arg_keys = jax.random.split(jax.random.key(seed), 4)
    return {
        "amplitudes": normal_values(arg_keys[0], (PAIRS, PAIR_TILES, PAIR_WIDTH), 1.0, 6.0, ((0, 8), (2, 4))),
        "integrals": normal_values(arg_keys[1], (BLOCKS, PAIR_WIDTH, PAIR_WIDTH), (BLK_PER_Q * PAIR_WIDTH) ** -0.5, 0.046875, ((1, 4), (2, 8))),
        "blocks": draw_blocks(jax.random.fold_in(arg_keys[3], 71), 0),
    }


def reference(amplitudes, integrals, blocks):
    running = jnp.zeros((PAIRS, PAIR_TILES, PAIR_WIDTH), jnp.float32)

    def add_block(which_block, running):
        row_tile = blocks[which_block, 0].astype(jnp.int32)
        col_tile = blocks[which_block, 1].astype(jnp.int32)
        left_rows = lax.dynamic_index_in_dim(amplitudes, row_tile, 1, keepdims=False).astype(jnp.float32)
        right_cols = lax.dynamic_index_in_dim(integrals, which_block, 0, keepdims=False).astype(jnp.float32)
        product = jnp.dot(left_rows, right_cols, preferred_element_type=jnp.float32)
        current = lax.dynamic_index_in_dim(running, col_tile, 1, keepdims=False)
        return lax.dynamic_update_index_in_dim(running, current + product, col_tile, 1)

    running = lax.fori_loop(jnp.int32(0), jnp.int32(BLOCKS), add_block, running)
    return running.astype(jnp.bfloat16)
```

```python
import functools

import jax
import jax.numpy as jnp
from jax import lax
from jax.experimental import pallas as pl
from jax.experimental.pallas import tpu as pltpu
from jax.sharding import PartitionSpec as P

MESH = pl.DeviceIdType.MESH
LAG = 2
STEPS = 32767.0


def flip(index, bit):
    return index + bit - 2 * bit * ((index // bit) % 2)


def kernel(
    sizes,
    order_ref,
    amp_ref,
    int_ref,
    out_ref,
    held_0,
    held_1,
    blocks_vmem,
    acc,
    fin,
    *rest,
):
    R, C, tiles, per = sizes
    levels = R.bit_length() - 1
    chips = C // 2
    keep = rest[0:levels]
    send_q = rest[levels : 2 * levels]
    recv_q = rest[2 * levels : 3 * levels]
    send_s = rest[3 * levels : 4 * levels]
    recv_s = rest[4 * levels : 5 * levels]
    (int_sem, own_sem, gsend, grecv, zq_send, zq_recv, zs_send, zs_recv,
     out_send, out_recv) = rest[5 * levels :]
    held = (held_0, held_1)
    chunks = 2 * tiles
    slab_rows = acc.shape[1]
    width = acc.shape[2]
    half_tiles = tiles // 2
    share = out_ref.shape[1]

    r = lax.axis_index("row")
    c = lax.axis_index("col")
    q = c // 2
    core = c % 2
    sibling = 2 * q + 1 - core

    blocks_copy = pltpu.make_async_copy(int_ref, blocks_vmem, int_sem)
    blocks_copy.start()

    barrier = pltpu.get_barrier_semaphore()
    for step in range(1, C):
        pl.semaphore_signal(
            barrier, inc=1, device_id=(r, (c + step) % C), device_id_type=MESH
        )
    for level in range(levels):
        pl.semaphore_signal(
            barrier, inc=1, device_id=(flip(r, 1 << level), c), device_id_type=MESH
        )
    pl.semaphore_wait(barrier, C - 1 + levels)

    def slot(h, v, who):
        return held[h].at[pl.ds(v * half_tiles, half_tiles), who]

    def push(h, v, who, target, number, own=False):
        source = amp_ref.at[h, pl.ds(v * half_tiles, half_tiles)] if own else slot(h, v, who)
        return pltpu.make_async_remote_copy(
            src_ref=source,
            dst_ref=slot(h, v, who),
            send_sem=gsend.at[h, v, number],
            recv_sem=grecv.at[h, v, number],
            device_id=(r, target),
            device_id_type=MESH,
        )

    def chip(k):
        there = q
        bit = 1
        while bit < chips:
            if k & bit:
                there = flip(there, bit)
            bit *= 2
        return 2 * there + core

    def to_sibling(h, v, k, own=False):
        return push(h, v, chip(k), sibling, chips + k, own)

    def same_core(h, v, k):
        return push(h, v, chip(k), chip(k), k)

    def own_copy(h):
        return pltpu.make_async_copy(
            amp_ref.at[h], held[h].at[:, c], own_sem.at[h]
        )

    relayed = chips == 4
    near = (1, 2) if relayed else tuple(range(1, chips))

    def send_own(h):
        for turn in range(2):
            for k in near:
                v = turn if k != 2 else 1 - turn
                push(h, v, c, chip(k), k, own=True).start()
        for v in range(2):
            to_sibling(h, v, 0, own=True).start()
        own_copy(h).start()

    def pass_near(h):
        for turn in range(2):
            for k in near:
                v = turn if k != 2 else 1 - turn
                same_core(h, v, k).wait_recv()
                if relayed and turn == 0:
                    push(h, v, chip(k), chip(3 - k), 3).start()
                to_sibling(h, v, k).start()

    def pass_far(h):
        if relayed:
            for v in range(2):
                same_core(h, v, 3).wait_recv()
                to_sibling(h, v, 3).start()

    def finish(h):
        own_copy(h).wait()
        for v in range(2):
            for k in range(chips):
                to_sibling(h, v, k).wait_recv()

    def finish_sends(h):
        for v in range(2):
            for number in range(1, 2 * chips):
                push(h, v, c, chip(1), number).wait_send()

    def z_copies(level, t):
        partner = (flip(r, 1 << level), c)
        return (
            pltpu.make_async_remote_copy(
                src_ref=send_q[level].at[t],
                dst_ref=recv_q[level].at[t],
                send_sem=zq_send.at[level, t],
                recv_sem=zq_recv.at[level, t],
                device_id=partner,
                device_id_type=MESH,
            ),
            pltpu.make_async_remote_copy(
                src_ref=send_s[level].at[t],
                dst_ref=recv_s[level].at[t],
                send_sem=zs_send.at[level, t],
                recv_sem=zs_recv.at[level, t],
                device_id=partner,
                device_id_type=MESH,
            ),
        )

    def exchange(level, t, get):
        bit = (r // (1 << level)) % 2
        for i in range(R >> (level + 1)):
            x = get(2 * i + 1 - bit)
            peak = jnp.maximum(jnp.max(jnp.abs(x), axis=0, keepdims=True), 1e-30)
            send_q[level][t, i] = jnp.round(x * (STEPS / peak)).astype(jnp.int32).astype(jnp.int16)
            send_s[level][t, i] = jnp.broadcast_to(peak * (1.0 / STEPS), (8, width))
        for copy in z_copies(level, t):
            copy.start()
        for i in range(R >> (level + 1)):
            keep[level][t, i] = get(2 * i + bit)

    def arrived(level, t):
        for copy in z_copies(level, t):
            copy.wait_recv()

        def get(i):
            scale = recv_s[level][t, i][0:1, :]
            coded = recv_q[level][t, i].astype(jnp.int32).astype(jnp.float32)
            return keep[level][t, i] + coded * scale

        return get

    def columns(who):
        return pl.ds(pl.multiple_of(who * width, width), width)

    def deliver(t):
        h, tile = t // tiles, t % tiles
        total = arrived(levels - 1, t)(0)
        fin[t] = total.astype(jnp.bfloat16).reshape(C // 2, share, width)
        for j in range(C // 2):
            target = 2 * j + h

            @pl.when(target != c)
            def _():
                pltpu.make_async_remote_copy(
                    src_ref=fin.at[t, j],
                    dst_ref=out_ref.at[tile, :, columns(c)],
                    send_sem=out_send,
                    recv_sem=out_recv,
                    device_id=(r, target),
                    device_id_type=MESH,
                ).start()

            @pl.when(target == c)
            def _():
                pltpu.make_async_copy(
                    fin.at[t, j], out_ref.at[tile, :, columns(c)], out_recv
                ).start()

    def multiply(h, tile, t):
        for j in range(per):
            block = order_ref[0, tile * per + j]
            pair_tile = order_ref[1, tile * per + j]
            left = held[h][pair_tile].reshape(R * slab_rows, -1)
            part = jnp.dot(
                left, blocks_vmem[block], preferred_element_type=jnp.float32
            ).reshape(R, slab_rows, width)
            if j == 0:
                acc[...] = part
            else:
                acc[...] += part
        exchange(0, t, lambda i: acc[i])

    def later(t):
        for level in range(1, levels):
            back = t - LAG * level

            @pl.when(jnp.logical_and(back >= 0, back < chunks))
            def _():
                exchange(level, back, arrived(level - 1, back))

        last = t - LAG * levels

        @pl.when(jnp.logical_and(last >= 0, last < chunks))
        def _():
            deliver(last)

    def run(h, lower, upper):
        @pl.loop(lower, upper)
        def _(tile):
            t = h * tiles + tile
            multiply(h, tile, t)
            later(t)

    send_own(0)
    pass_near(0)
    send_own(1)
    pass_far(0)
    finish(0)
    blocks_copy.wait()
    run(0, 0, tiles // 2)
    pass_near(1)
    run(0, tiles // 2, tiles)
    pass_far(1)
    finish(1)
    run(1, 0, tiles)

    @pl.loop(chunks, chunks + LAG * levels)
    def _(t):
        later(t)

    finish_sends(0)
    finish_sends(1)
    for level in range(levels):

        @pl.loop(0, chunks)
        def _(t):
            for copy in z_copies(level, t):
                copy.wait_send()

    rest_of = out_ref.at[:, :, pl.ds(0, (C - 1) * width)]
    pltpu.make_async_copy(rest_of, rest_of, out_send).wait()
    pltpu.make_async_copy(out_ref, out_ref, out_recv).wait()


def on_device(R, C, amplitudes, integrals, blocks):
    pairs, tiles, inner = amplitudes.shape
    count, _, width = integrals.shape
    per = count // tiles
    levels = R.bit_length() - 1
    share = pairs * C // (R * C)
    groups = pairs // share
    chunks = 2 * tiles
    slab_rows = pairs * C // R // 2

    key = blocks[:, 1] * count + jnp.arange(count, dtype=jnp.int32)
    rank = jnp.sum((key[:, None] > key[None, :]).astype(jnp.int32), axis=1)
    at = rank[:, None] == jnp.arange(count, dtype=jnp.int32)[None, :]
    both = jnp.stack([jnp.arange(count, dtype=jnp.int32), blocks[:, 0]], axis=0)
    order = jnp.sum(jnp.where(at[None], both[:, :, None], 0), axis=1)

    halves = amplitudes.reshape(groups // 2, 2, share, tiles, inner)
    halves = halves.transpose(1, 3, 0, 2, 4).reshape(2, tiles, pairs // 2, inner)

    held = pltpu.VMEM((tiles, C, pairs // 2, inner), jnp.bfloat16)
    parts = [R >> (level + 1) for level in range(levels)]
    coded = [pltpu.VMEM((chunks, n, slab_rows, width), jnp.int16) for n in parts]
    scales = [pltpu.VMEM((chunks, n, 8, width), jnp.float32) for n in parts]
    dma = pltpu.SemaphoreType.DMA
    out = pl.pallas_call(
        functools.partial(kernel, (R, C, tiles, per)),
        out_shape=jax.ShapeDtypeStruct((tiles, share, C * width), jnp.bfloat16),
        in_specs=[
            pl.BlockSpec(memory_space=pltpu.SMEM),
            pl.BlockSpec(memory_space=pl.ANY),
            pl.BlockSpec(memory_space=pl.ANY),
        ],
        out_specs=pl.BlockSpec(memory_space=pltpu.VMEM),
        scratch_shapes=[
            held,
            held,
            pltpu.VMEM(integrals.shape, jnp.bfloat16),
            pltpu.VMEM((R, slab_rows, width), jnp.float32),
            pltpu.VMEM((chunks, C // 2, share, width), jnp.bfloat16),
        ]
        + [pltpu.VMEM((chunks, n, slab_rows, width), jnp.float32) for n in parts]
        + coded
        + coded
        + scales
        + scales
        + [
            dma,
            dma((2,)),
            dma((2, 2, C)),
            dma((2, 2, C)),
            dma((levels, chunks)),
            dma((levels, chunks)),
            dma((levels, chunks)),
            dma((levels, chunks)),
            dma,
            dma,
        ],
        compiler_params=pltpu.CompilerParams(
            collective_id=0, has_side_effects=True, vmem_limit_bytes=67043328
        ),
    )(order, halves, integrals)
    return out.transpose(1, 0, 2)


def solution(mesh):
    return jax.shard_map(
        functools.partial(on_device, mesh.shape["row"], mesh.shape["col"]),
        mesh=mesh,
        in_specs=(P("col", None, "row"), P(None, "row", "col"), P()),
        out_specs=P(("row", "col"), None, None),
        check_vma=False,
    )
```
